32 devices in a mesh: ctx: 16 (over z, x, core), head: 2 (over y).
Axes of the slice: x: 2, y: 2, z: 4, core: 2. Of those that a mesh axis runs over, the one named last changes fastest.
Arguments:
- q_absorbed: bfloat16 [2048, 64, 576], P('ctx', 'head'), may hold values from -6 to 6
- grad_out: bfloat16 [2048, 64, 512], P('ctx', 'head'), may hold values from -6 to 6
- log_norm: float32 [2048, 64], P('ctx', 'head'), may hold values from 5 to 7
- out_dot: float32 [2048, 64], P('ctx', 'head'), may hold values from -6 to 6
- kv_cache: bfloat16 [2048, 576], P(('ctx', 'head')), may hold values from -6 to 6
- block_links: int32 [16, 4], P('ctx'), may hold values 0 or 1
Outputs:
- d_query: bfloat16 [2048, 64, 576], P('ctx', 'head')
- d_kv: bfloat16 [2048, 576], P(('ctx', 'head'))
The draws below stay inside these ranges and needn't reach their ends.
All inputs are finite; a program needn't handle non-finite values. No bound on the sum of `block_links` on one device may be relied on, other than what follows from the above.
Results may differ from the reference program's by a relative error of at most 0.0061.
Values may be sent and summed in bfloat16 or wider, within the bound.
A program may use at most 128 MiB of HBM per device.

```python
import jax
import jax.numpy as jnp
from jax import lax

LAT = 512
ROPE = 64
HEADS = 64
OFFS = 4
TOK_DEV = 128
TOKENS = 2048
N_CTX = 16


def place_ends(array, own_key, low, high):
    index_at = [jax.random.randint(jax.random.fold_in(own_key, axis), (), 0, length) for axis, length in enumerate(array.shape)]
    main_axis = array.shape.index(max(array.shape))
    neighbour = index_at[:main_axis] + [(index_at[main_axis] + 1) % array.shape[main_axis]] + index_at[main_axis + 1:]
    return array.at[tuple(index_at)].set(low).at[tuple(neighbour)].set(high)


def block_levels(rng, extent, shards, low, top_value):
    gain, own = 1.0, jax.random.fold_in(rng, 6)
    for dim, shards_of in shards:
        heights = jnp.exp(jax.random.uniform(jax.random.fold_in(own, dim), (shards_of,), jnp.float32, low / len(shards), top_value / len(shards)))
        gain = gain * jnp.repeat(heights, extent[dim] // shards_of).reshape([-1 if axis == dim else 1 for axis in range(len(extent))])
    return gain


def normal_values(own_key, extent, scale, limit, shards=(), held_as=jnp.bfloat16):
    entries = scale * jax.random.normal(own_key, extent, jnp.float32)
    if shards:
        entries = entries * block_levels(own_key, extent, shards, -0.22, 0.18)
    return jnp.clip(entries, -limit, limit).astype(held_as)


def setup_inputs(seed: int = 0) -> dict:
    key_list = jax.random.split(jax.random.key(seed), 7)
    q_absorbed = normal_values(key_list[0], (TOKENS, HEADS, LAT + ROPE), 1.0, 6.0, ((0, 16), (1, 2)))
    grad_out = normal_values(key_list[1], (TOKENS, HEADS, LAT), 1.0, 6.0, ((0, 16), (1, 2)))
    log_norm = jnp.clip(5.0 + 2.0 * jax.random.uniform(key_list[2], (TOKENS, HEADS), jnp.float32) ** block_levels(key_list[2], (TOKENS, HEADS), ((0, 16), (1, 2)), -0.2, 0.2), 5.0, 7.0)
    out_dot = normal_values(key_list[3], (TOKENS, HEADS), 1.0, 6.0, ((0, 16), (1, 2)), jnp.float32)
    kv_cache = normal_values(key_list[4], (TOKENS, LAT + ROPE), 1.0, 6.0, ((0, 32),))
    block_links = place_ends((jax.random.randint(key_list[5], (N_CTX, OFFS), 0, 4) < 3).astype(jnp.int32), jax.random.fold_in(key_list[5], 1), 0, 1)
    return dict(q_absorbed=q_absorbed, grad_out=grad_out, log_norm=log_norm, out_dot=out_dot, kv_cache=kv_cache, block_links=block_links)


offset_list = (0, 1, 2, 8)


def block_terms(query_rows, grad_rows, norm_rows, dot_rows, key_rows, live_flag, causal):
    lat_width = grad_rows.shape[2]
    score_scale = query_rows.shape[2] ** -0.5
    query_f32 = query_rows.astype(jnp.float32)
    grad_f32 = grad_rows.astype(jnp.float32)
    key_f32 = key_rows.astype(jnp.float32)
    scores = jnp.einsum("thc,kc->thk", query_f32, key_f32) * score_scale
    keep_mask = jnp.broadcast_to(live_flag > 0, scores.shape)
    if causal:
        row_pos = lax.broadcasted_iota(jnp.int32, scores.shape, 0)
        col_pos = lax.broadcasted_iota(jnp.int32, scores.shape, 2)
        keep_mask = keep_mask & (row_pos >= col_pos)
    attn_prob = jnp.where(keep_mask, jnp.exp(scores - norm_rows[:, :, None]), 0.0)
    grad_prob = jnp.einsum("thl,kl->thk", grad_f32, key_f32[:, :lat_width])
    grad_score = (attn_prob * (grad_prob - dot_rows[:, :, None]) * score_scale).astype(jnp.bfloat16).astype(jnp.float32)
    prob_rounded = attn_prob.astype(jnp.bfloat16).astype(jnp.float32)
    query_term = jnp.einsum("thk,kc->thc", grad_score, key_f32)
    key_term = jnp.einsum("thk,thc->kc", grad_score, query_f32)
    value_term = jnp.einsum("thk,thl->kl", prob_rounded, grad_f32)
    key_term = key_term + jnp.pad(value_term, ((0, 0), (0, key_rows.shape[1] - lat_width)))
    return query_term, key_term


def reference(q_absorbed, grad_out, log_norm, out_dot, kv_cache, block_links):
    def one_block(block, carry):
        grads_q, grads_kv = carry
        start_row = (block * TOK_DEV).astype(jnp.int32)
        query_rows = lax.dynamic_slice_in_dim(q_absorbed, start_row, TOK_DEV, 0)
        grad_rows = lax.dynamic_slice_in_dim(grad_out, start_row, TOK_DEV, 0)
        norm_rows = lax.dynamic_slice_in_dim(log_norm, start_row, TOK_DEV, 0)
        dot_rows = lax.dynamic_slice_in_dim(out_dot, start_row, TOK_DEV, 0)
        summed = jnp.zeros(query_rows.shape, jnp.float32)
        for position, offset in enumerate(offset_list):
            source = (((block - offset) % N_CTX) * TOK_DEV).astype(jnp.int32)
            key_rows = lax.dynamic_slice_in_dim(kv_cache, source, TOK_DEV, 0)
            query_term, key_term = block_terms(query_rows, grad_rows, norm_rows, dot_rows, key_rows, block_links[block, position], offset == 0)
            summed = summed + query_term
            current = lax.dynamic_slice_in_dim(grads_kv, source, TOK_DEV, 0)
            grads_kv = lax.dynamic_update_slice_in_dim(grads_kv, current + key_term, source, 0)
        grads_q = lax.dynamic_update_slice_in_dim(grads_q, summed.astype(jnp.bfloat16), start_row, 0)
        return grads_q, grads_kv

    initial = (jnp.zeros(q_absorbed.shape, jnp.bfloat16), jnp.zeros(kv_cache.shape, jnp.float32))
    grads_q, grads_kv = lax.fori_loop(0, N_CTX, one_block, initial)
    return grads_q, grads_kv.astype(jnp.bfloat16)
```

```python
import functools
import math

import jax
import jax.numpy as jnp
from jax import lax
from jax.experimental import pallas as pl
from jax.experimental.pallas import tpu as pltpu
from jax.sharding import PartitionSpec as P

offset_list = (0, 1, 2, 8)
F32 = jnp.float32
BF16 = jnp.bfloat16


def dot(a, b, ca, cb):
    return lax.dot_general(a, b, (((ca,), (cb,)), ((), ())), preferred_element_type=F32)


def compute_kernel(heads, links, kv_ref, q_ref, g_ref, ln_ref, od_ref, dq_ref, dkv_ref, acc):
    step = pl.program_id(0)
    rows, feat = q_ref.shape
    lat = g_ref.shape[1]
    scale = feat ** (-0.5)
    log2e = math.log2(math.e)
    q = q_ref[...]
    g = g_ref[...]
    ln = ln_ref[...] * log2e
    od = od_ref[...]
    n_off, blk, _ = kv_ref.shape
    kv = kv_ref[...].reshape(n_off * blk, feat)
    s = dot(kv, q, 1, 1)
    dp = dot(kv[:, :lat], g, 1, 1)
    ps, dss = [], []
    for pos in range(n_off):
        sl = slice(pos * blk, (pos + 1) * blk)
        bias = jnp.where(links[0, pos] > 0, ln, 1e30)
        p = jnp.exp2(s[sl] * (scale * log2e) - bias)
        if offset_list[pos] == 0:
            key = lax.broadcasted_iota(jnp.int32, p.shape, 0)
            row = lax.broadcasted_iota(jnp.int32, p.shape, 1) + step * rows
            p = jnp.where(row >= key * heads, p, 0.0)
        ps.append(p.astype(BF16))
        dss.append((p * (dp[sl] - od) * scale).astype(BF16))
    pb = jnp.concatenate(ps, 0)
    ds = jnp.concatenate(dss, 0)
    dq_ref[...] = dot(ds, kv, 0, 0).astype(BF16)
    dk = dot(ds, q, 1, 0)
    dv = dot(pb, g, 1, 0)

    @pl.when(step == 0)
    def _():
        acc[...] = jnp.zeros_like(acc)

    acc[:, :lat] += dk[:, :lat] + dv
    acc[:, lat:] += dk[:, lat:]

    @pl.when(step == pl.num_programs(0) - 1)
    def _():
        dkv_ref[...] = acc[...].astype(dkv_ref.dtype).reshape(dkv_ref.shape)


def compute(q, g, ln, od, kv, links, tile=512):
    toks, heads, feat = q.shape
    lat = g.shape[2]
    rows = toks * heads
    n_off, blk, _ = kv.shape
    tile = min(tile, rows)
    dq, dkv = pl.pallas_call(
        functools.partial(compute_kernel, heads),
        grid=(rows // tile,),
        in_specs=[
            pl.BlockSpec(memory_space=pltpu.SMEM),
            pl.BlockSpec((n_off, blk, feat), lambda i: (0, 0, 0)),
            pl.BlockSpec((tile, feat), lambda i: (i, 0)),
            pl.BlockSpec((tile, lat), lambda i: (i, 0)),
            pl.BlockSpec((1, tile), lambda i: (0, i)),
            pl.BlockSpec((1, tile), lambda i: (0, i)),
        ],
        out_specs=[
            pl.BlockSpec((tile, feat), lambda i: (i, 0)),
            pl.BlockSpec((n_off, blk, feat), lambda i: (0, 0, 0)),
        ],
        out_shape=[
            jax.ShapeDtypeStruct((rows, feat), BF16),
            jax.ShapeDtypeStruct((n_off, blk, feat), F32),
        ],
        scratch_shapes=[pltpu.VMEM((n_off * blk, feat), F32)],
        compiler_params=pltpu.CompilerParams(dimension_semantics=("arbitrary",), vmem_limit_bytes=48 << 20),
        name="mla_bwd",
    )(links, kv, q.reshape(rows, feat), g.reshape(rows, lat), ln.reshape(1, rows), od.reshape(1, rows))
    return dq.reshape(toks, heads, feat), dkv


def from_behind(array, axis, by):
    length = lax.axis_size(axis)
    return lax.ppermute(array, axis, [(i, (i + by) % length) for i in range(length)])


def shards(q, g, ln, od, kv, links):
    own = lax.all_gather(kv, "head", axis=0, tiled=True)
    keys = jnp.stack([own] + [from_behind(own, "ctx", o) for o in offset_list[1:]])
    dq, part = compute(q, g, ln, od, keys, links)
    total = part[0]
    for pos in range(1, len(offset_list)):
        total = total + from_behind(part[pos].astype(BF16), "ctx", -offset_list[pos]).astype(F32)
    dkv = lax.psum_scatter(total, "head", scatter_dimension=0, tiled=True)
    return dq, dkv.astype(BF16)


def solution(mesh):
    in_specs = (
        P("ctx", "head", None),
        P("ctx", "head", None),
        P("ctx", "head"),
        P("ctx", "head"),
        P(("ctx", "head"), None),
        P("ctx", None),
    )
    out_specs = (P("ctx", "head", None), P(("ctx", "head"), None))
    return jax.shard_map(shards, mesh=mesh, in_specs=in_specs, out_specs=out_specs, check_vma=False)
```

```python
import functools
import math

import jax
import jax.numpy as jnp
from jax import lax
from jax.experimental import pallas as pl
from jax.experimental.pallas import tpu as pltpu
from jax.sharding import PartitionSpec as P

offset_list = (0, 1, 2, 8)
F32 = jnp.float32
BF16 = jnp.bfloat16


def dot(a, b, ca, cb):
    return lax.dot_general(a, b, (((ca,), (cb,)), ((), ())), preferred_element_type=F32)


def compute_kernel(n_head, head_at, links, kv_ref, q_ref, g_ref, ln_ref, od_ref, dq_ref, own_ref, away_ref, acc):
    step = pl.program_id(0)
    group, feat, toks = q_ref.shape
    lat = g_ref.shape[2]
    scale = feat ** (-0.5)
    log2e = math.log2(math.e)
    cols = group * toks
    q = jnp.concatenate([q_ref[i] for i in range(group)], 1)
    g = g_ref[...].reshape(cols, lat)
    ln = jnp.concatenate([ln_ref[0, i : i + 1, :] for i in range(group)], 1) * log2e
    od = jnp.concatenate([od_ref[0, i : i + 1, :] for i in range(group)], 1)
    n_off, _, part, _ = kv_ref.shape
    blk = n_head * part
    kv = kv_ref[...].reshape(n_off * blk, feat)
    s = dot(kv, q, 1, 0)
    dp = dot(kv[:, :lat], g, 1, 1)
    ps, dss = [], []
    for pos in range(n_off):
        sl = slice(pos * blk, (pos + 1) * blk)
        bias = jnp.where(links[0, pos] > 0, ln, 1e30)
        p = jnp.exp2(s[sl] * (scale * log2e) - bias)
        if offset_list[pos] == 0:
            key = lax.broadcasted_iota(jnp.int32, p.shape, 0) + head_at[0] * part
            key = jnp.where(key >= blk, key - blk, key)
            tok = lax.rem(lax.broadcasted_iota(jnp.int32, p.shape, 1), toks)
            p = jnp.where(tok >= key, p, 0.0)
        ps.append(p.astype(BF16))
        dss.append((p * (dp[sl] - od) * scale).astype(BF16))
    pb = jnp.concatenate(ps, 0)
    ds = jnp.concatenate(dss, 0)
    dq = dot(kv, ds, 0, 0).astype(BF16)
    for i in range(group):
        dq_ref[i] = dq[:, i * toks : (i + 1) * toks]
    dk = dot(ds, q, 1, 1)
    dv = dot(pb, g, 1, 0)

    @pl.when(step == 0)
    def _():
        acc[...] = jnp.zeros_like(acc)

    acc[:, :lat] += dk[:, :lat] + dv
    acc[:, lat:] += dk[:, lat:]

    @pl.when(step == pl.num_programs(0) - 1)
    def _():
        total = acc[...].reshape(n_off, n_head, part, feat)
        own_ref[...] = total[:, 0]
        away_ref[...] = total[:, 1:].astype(BF16)


def compute(n_head, q, g, ln, od, kv, links, group=4):
    heads, feat, toks = q.shape
    lat = g.shape[2]
    n_off, _, part, _ = kv.shape
    group = math.gcd(group, heads)
    steps = heads // group
    head_at = lax.axis_index("head").astype(jnp.int32).reshape(1)
    return pl.pallas_call(
        functools.partial(compute_kernel, n_head),
        grid=(steps,),
        in_specs=[
            pl.BlockSpec(memory_space=pltpu.SMEM),
            pl.BlockSpec(memory_space=pltpu.SMEM),
            pl.BlockSpec(kv.shape, lambda i: (0, 0, 0, 0)),
            pl.BlockSpec((group, feat, toks), lambda i: (i, 0, 0)),
            pl.BlockSpec((group, toks, lat), lambda i: (i, 0, 0)),
            pl.BlockSpec((1, group, toks), lambda i: (i, 0, 0)),
            pl.BlockSpec((1, group, toks), lambda i: (i, 0, 0)),
        ],
        out_specs=[
            pl.BlockSpec((group, feat, toks), lambda i: (i, 0, 0)),
            pl.BlockSpec((n_off, part, feat), lambda i: (0, 0, 0)),
            pl.BlockSpec((n_off, n_head - 1, part, feat), lambda i: (0, 0, 0, 0)),
        ],
        out_shape=[
            jax.ShapeDtypeStruct((heads, feat, toks), BF16),
            jax.ShapeDtypeStruct((n_off, part, feat), F32),
            jax.ShapeDtypeStruct((n_off, n_head - 1, part, feat), BF16),
        ],
        scratch_shapes=[pltpu.VMEM((n_off * n_head * part, feat), F32)],
        compiler_params=pltpu.CompilerParams(dimension_semantics=("arbitrary",), vmem_limit_bytes=48 << 20),
        cost_estimate=pl.CostEstimate(flops=12 * 10**9, bytes_accessed=14 * 10**6, transcendentals=2 * 10**6),
        name="mla_bwd",
    )(head_at, links, kv, q, g, ln.reshape(steps, group, toks), od.reshape(steps, group, toks))


def from_behind(array, axis, by):
    length = lax.axis_size(axis)
    return lax.ppermute(array, axis, [(i, (i + by) % length) for i in range(length)])


def shards(q, g, ln, od, kv, links):
    n_head = lax.axis_size("head")
    mine = [kv] + [from_behind(kv, "ctx", o) for o in offset_list[1:]]
    keys = jnp.stack([jnp.stack([m] + [from_behind(m, "head", -j) for j in range(1, n_head)]) for m in mine])
    dq, own, away = compute(
        n_head,
        jnp.transpose(q, (1, 2, 0)),
        jnp.transpose(g, (1, 0, 2)),
        ln.T,
        od.T,
        keys,
        links,
    )
    for j in range(1, n_head):
        own = own + from_behind(away[:, j - 1], "head", j).astype(F32)
    total = own[0]
    for pos in range(1, len(offset_list)):
        total = total + from_behind(own[pos].astype(BF16), "ctx", -offset_list[pos]).astype(F32)
    return jnp.transpose(dq, (2, 0, 1)), total.astype(BF16)


def solution(mesh):
    in_specs = (
        P("ctx", "head", None),
        P("ctx", "head", None),
        P("ctx", "head"),
        P("ctx", "head"),
        P(("ctx", "head"), None),
        P("ctx", None),
    )
    out_specs = (P("ctx", "head", None), P(("ctx", "head"), None))
    return jax.shard_map(shards, mesh=mesh, in_specs=in_specs, out_specs=out_specs, check_vma=False)
```

```python
import functools
import math

import jax
import jax.numpy as jnp
from jax import lax
from jax.experimental import pallas as pl
from jax.experimental.pallas import tpu as pltpu
from jax.sharding import PartitionSpec as P

offset_list = (0, 1, 2, 8)
F32 = jnp.float32
BF16 = jnp.bfloat16


def dot(a, b, ca, cb):
    return lax.dot_general(a, b, (((ca,), (cb,)), ((), ())), preferred_element_type=F32)


MESH = pl.DeviceIdType.MESH
FIRST, LAST = (0, 2), (2, 4)


def fused_kernel(
    n_ctx, n_head, links, kv_ref, q_hbm, g_hbm, ln_ref, od_ref,
    dq_hbm, dkv_ref,
    qv, graw, gwide, gv, dsv, pbv, dqv, acc, kvbuf, away, yrecv, fwd, crecv,
    q_sem, g_sem, dq_sem, gs_s, gs_r, fw_s, fw_r, ry_s, ry_r, rc_s, rc_r,
):
    me = lax.axis_index("ctx")
    head = lax.axis_index("head")
    steps, group, feat, toks = qv.shape
    chunks, width, heads, lat = graw.shape
    cols = group * toks
    n_off, _, part, _ = kvbuf.shape
    blk = n_head * part
    scale = feat ** (-0.5)
    log2e = math.log2(math.e)

    def load_g(i):
        return pltpu.make_async_copy(g_hbm.at[pl.ds(i * width, width)], graw.at[i], g_sem.at[i])

    def load_q(i):
        return pltpu.make_async_copy(q_hbm.at[pl.ds(i * group, group)], qv.at[i], q_sem.at[i])

    def store_dq(i):
        return pltpu.make_async_copy(dqv.at[i], dq_hbm.at[pl.ds(i * group, group)], dq_sem.at[i])

    def loop(count, body):
        def run(i, carry):
            body(i)
            return carry

        lax.fori_loop(0, count, run, 0)

    def at_ctx(by):
        return (lax.rem(me + by + n_ctx, n_ctx), head)

    def at_head(by):
        return (me, lax.rem(head + by + n_head, n_head))

    def send(src, dst, s_sem, r_sem, where):
        return pltpu.make_async_remote_copy(
            src_ref=src, dst_ref=dst, send_sem=s_sem, recv_sem=r_sem, device_id=where, device_id_type=MESH
        )

    loop(chunks, lambda i: load_g(i).start())

    away_by = sorted({by % n_ctx for o in offset_list[1:] for by in (o, -o)})
    barrier = pltpu.get_barrier_semaphore()
    for by in away_by:
        pl.semaphore_signal(barrier, inc=1, device_id=at_ctx(by), device_id_type=MESH)
    for j in range(1, n_head):
        pl.semaphore_signal(barrier, inc=1, device_id=at_head(j), device_id_type=MESH)
    pl.semaphore_wait(barrier, len(away_by) + n_head - 1)

    gather = [
        send(kv_ref, kvbuf.at[pos, 0], gs_s.at[pos - 1], gs_r.at[pos - 1], at_ctx(offset_list[pos]))
        for pos in range(1, n_off)
    ]
    spread = [
        [
            send(kv_ref if pos == 0 else kvbuf.at[pos, 0], kvbuf.at[pos, j],
                 fw_s.at[pos, j - 1], fw_r.at[pos, j - 1], at_head(-j))
            for j in range(1, n_head)
        ]
        for pos in range(n_off)
    ]
    for copy in gather:
        copy.start()
    for copy in spread[0]:
        copy.start()
    loop(steps, lambda i: load_q(i).start())
    kvbuf[0, 0] = kv_ref[...]

    def relayout(i):
        load_g(i).wait()
        wide = graw[i].reshape(width * heads, lat).astype(F32)
        lanes = gwide.shape[2]
        for c in range(gwide.shape[0]):
            gwide[c] = wide[:, c * lanes : (c + 1) * lanes]
        for h in range(heads):
            for c in range(gwide.shape[0]):
                gv[h // group, h % group, pl.ds(i * width, width), c * lanes : (c + 1) * lanes] = gwide[
                    c, pl.ds(h, width, stride=heads), :
                ].astype(BF16)

    loop(chunks, relayout)

    def scores(i, low, high):
        keys = kvbuf[low:high].reshape((high - low) * blk, feat)
        q = jnp.concatenate([qv[i, k] for k in range(group)], 1)
        g = gv[i].reshape(cols, lat)
        ln = jnp.concatenate([ln_ref[i, k : k + 1, :] for k in range(group)], 1) * log2e
        od = jnp.concatenate([od_ref[i, k : k + 1, :] for k in range(group)], 1)
        s = dot(keys, q, 1, 0)
        dp = dot(keys[:, :lat], g, 1, 1)
        ps, dss = [], []
        for pos in range(low, high):
            sl = slice((pos - low) * blk, (pos - low + 1) * blk)
            bias = jnp.where(links[0, pos] > 0, ln, 1e30)
            p = jnp.exp2(s[sl] * (scale * log2e) - bias)
            if offset_list[pos] == 0:
                key = lax.broadcasted_iota(jnp.int32, p.shape, 0) + head * part
                key = jnp.where(key >= blk, key - blk, key)
                tok = lax.rem(lax.broadcasted_iota(jnp.int32, p.shape, 1), toks)
                p = jnp.where(tok >= key, p, 0.0)
            ps.append(p.astype(BF16))
            dss.append((p * (dp[sl] - od) * scale).astype(BF16))
        return jnp.concatenate(ps, 0), jnp.concatenate(dss, 0), q, g

    def key_terms(pb, ds, q, g, low, high):
        rows = slice(low * blk, high * blk)
        dk = dot(ds, q, 1, 1)
        dv = dot(pb, g, 1, 0)
        acc[rows, :lat] += dk[:, :lat] + dv
        acc[rows, lat:] += dk[:, lat:]

    def across(low, high, slot):
        return [
            send(away.at[j - 1, low:high], yrecv.at[j - 1, low:high], ry_s.at[slot, j - 1],
                 ry_r.at[slot, j - 1], at_head(j))
            for j in range(1, n_head)
        ]

    def pack(low, high):
        for pos in range(low, high):
            for j in range(1, n_head):
                start = pos * blk + j * part
                away[j - 1, pos] = acc[start : start + part, :].astype(BF16)

    def folded(pos):
        total = acc[pos * blk : pos * blk + part, :]
        for j in range(1, n_head):
            total = total + yrecv[j - 1, pos].astype(F32)
        return total

    back = [
        send(fwd.at[pos - 1], crecv.at[pos - 1], rc_s.at[pos - 1], rc_r.at[pos - 1], at_ctx(-offset_list[pos]))
        for pos in range(1, n_off)
    ]

    acc[...] = jnp.zeros_like(acc)
    for pos in range(1, n_off):
        if pos == FIRST[1]:
            arrive(spread, FIRST)
            first_scores(loop, steps, load_q, scores, dsv, pbv, blk)
        gather[pos - 1].wait_recv()
        for copy in spread[pos]:
            copy.start()
    arrive(spread, LAST)

    def second(i):
        pb, ds, q, g = scores(i, *LAST)
        dsv[i, LAST[0] * blk : LAST[1] * blk, :] = ds
        key_terms(pb, ds, q, g, *LAST)

    loop(steps, second)
    pack(*LAST)

    def third(i):
        q = jnp.concatenate([qv[i, k] for k in range(group)], 1)
        key_terms(pbv[i], dsv[i, : FIRST[1] * blk, :], q, gv[i].reshape(cols, lat), *FIRST)

    def fourth(i):
        keys = kvbuf[...].reshape(n_off * blk, feat)
        dq = dot(keys, dsv[i], 0, 0).astype(BF16)
        for k in range(group):
            dqv[i, k] = dq[:, k * toks : (k + 1) * toks]
        store_dq(i).start()

    far, near = across(*LAST, 1), across(*FIRST, 0)
    for copy in far:
        copy.start()
    loop(steps, third)
    for copy in far:
        copy.wait_recv()
    for pos in range(*LAST):
        fwd[pos - 1] = folded(pos).astype(BF16)
    pack(*FIRST)
    for pos in range(*LAST):
        back[pos - 1].start()
    for copy in near:
        copy.start()
    loop(steps, fourth)
    for copy in near:
        copy.wait_recv()
    for pos in range(1, FIRST[1]):
        fwd[pos - 1] = folded(pos).astype(BF16)
    total = folded(0)
    for pos in range(1, FIRST[1]):
        back[pos - 1].start()
    loop(steps, lambda i: store_dq(i).wait())
    for copy in gather + sum(spread, []) + far + near:
        copy.wait_send()
    for copy in back[::-1]:
        copy.wait()
    for pos in range(1, n_off):
        total = total + crecv[pos - 1].astype(F32)
    dkv_ref[...] = total.astype(BF16)


def arrive(spread, span):
    for pos in range(*span):
        for copy in spread[pos]:
            copy.wait_recv()


def first_scores(loop, steps, load_q, scores, dsv, pbv, blk):
    def first(i):
        load_q(i).wait()
        pb, ds, _, _ = scores(i, *FIRST)
        dsv[i, : FIRST[1] * blk, :] = ds
        pbv[i] = pb

    loop(steps, first)


def fused(n_ctx, n_head, q, g, ln, od, kv, links, group=4, width=32):
    heads, feat, toks = q.shape
    lat = g.shape[2]
    part = kv.shape[0]
    n_off = len(offset_list)
    group = math.gcd(group, heads)
    width = math.gcd(width, toks)
    steps, chunks = heads // group, toks // width
    cols, keys = group * toks, n_off * n_head * part
    near = FIRST[1] * n_head * part
    dma = pltpu.SemaphoreType.DMA
    hbm = pl.BlockSpec(memory_space=pl.ANY)
    vmem = pl.BlockSpec(memory_space=pltpu.VMEM)
    return pl.pallas_call(
        functools.partial(fused_kernel, n_ctx, n_head),
        in_specs=[pl.BlockSpec(memory_space=pltpu.SMEM), vmem, hbm, hbm, vmem, vmem],
        out_specs=[hbm, vmem],
        out_shape=[
            jax.ShapeDtypeStruct((heads, feat, toks), BF16),
            jax.ShapeDtypeStruct((part, feat), BF16),
        ],
        scratch_shapes=[
            pltpu.VMEM((steps, group, feat, toks), BF16),
            pltpu.VMEM((chunks, width, heads, lat), BF16),
            pltpu.VMEM((lat // 128, width * heads, 128), F32),
            pltpu.VMEM((steps, group, toks, lat), BF16),
            pltpu.VMEM((steps, keys, cols), BF16),
            pltpu.VMEM((steps, near, cols), BF16),
            pltpu.VMEM((steps, group, feat, toks), BF16),
            pltpu.VMEM((keys, feat), F32),
            pltpu.VMEM((n_off, n_head, part, feat), BF16),
            pltpu.VMEM((n_head - 1, n_off, part, feat), BF16),
            pltpu.VMEM((n_head - 1, n_off, part, feat), BF16),
            pltpu.VMEM((n_off - 1, part, feat), BF16),
            pltpu.VMEM((n_off - 1, part, feat), BF16),
            dma((steps,)),
            dma((chunks,)),
            dma((steps,)),
            dma((n_off - 1,)),
            dma((n_off - 1,)),
            dma((n_off, n_head - 1)),
            dma((n_off, n_head - 1)),
            dma((2, n_head - 1)),
            dma((2, n_head - 1)),
            dma((n_off - 1,)),
            dma((n_off - 1,)),
        ],
        compiler_params=pltpu.CompilerParams(
            collective_id=0, has_side_effects=True, vmem_limit_bytes=56 << 20
        ),
        cost_estimate=pl.CostEstimate(flops=12 * 10**9, bytes_accessed=14 * 10**6, transcendentals=2 * 10**6),
        name="mla_bwd",
    )(links, kv, q, g, ln.reshape(steps, group, toks), od.reshape(steps, group, toks))


def shards(q, g, ln, od, kv, links):
    dq, dkv = fused(
        lax.axis_size("ctx"),
        lax.axis_size("head"),
        jnp.transpose(q, (1, 2, 0)),
        g,
        ln.T,
        od.T,
        kv,
        links,
    )
    return jnp.transpose(dq, (2, 0, 1)), dkv


def solution(mesh):
    in_specs = (
        P("ctx", "head", None),
        P("ctx", "head", None),
        P("ctx", "head"),
        P("ctx", "head"),
        P(("ctx", "head"), None),
        P("ctx", None),
    )
    out_specs = (P("ctx", "head", None), P(("ctx", "head"), None))
    return jax.shard_map(shards, mesh=mesh, in_specs=in_specs, out_specs=out_specs, check_vma=False)
```

```python
import functools
import math

import jax
import jax.numpy as jnp
from jax import lax
from jax.experimental import pallas as pl
from jax.experimental.pallas import tpu as pltpu
from jax.sharding import PartitionSpec as P

offset_list = (0, 1, 2, 8)
F32 = jnp.float32
BF16 = jnp.bfloat16


def dot(a, b, ca, cb):
    return lax.dot_general(a, b, (((ca,), (cb,)), ((), ())), preferred_element_type=F32)


MESH = pl.DeviceIdType.MESH
FIRST, LAST = (0, 2), (2, 4)


def fused_kernel(
    n_ctx, n_head, links, kv_ref, q_hbm, g_hbm, ln_ref, od_ref,
    dqv, dkv_ref,
    qv, graw, gwide, gv, dsv, pbv, acc, kvbuf, away, yrecv, fwd, crecv,
    q_sem, g_sem, gs_s, gs_r, fw_s, fw_r, ry_s, ry_r, rc_s, rc_r,
):
    me = lax.axis_index("ctx")
    head = lax.axis_index("head")
    steps, group, feat, toks = qv.shape
    chunks, width, heads, lat = graw.shape
    cols = group * toks
    n_off, _, part, _ = kvbuf.shape
    blk = n_head * part
    scale = feat ** (-0.5)
    log2e = math.log2(math.e)

    def load_g(i):
        return pltpu.make_async_copy(g_hbm.at[pl.ds(i * width, width)], graw.at[i], g_sem.at[i])

    def load_q(i):
        return pltpu.make_async_copy(q_hbm.at[pl.ds(i * group, group)], qv.at[i], q_sem.at[i])

    def loop(count, body, start=0):
        def run(i, carry):
            body(i)
            return carry

        lax.fori_loop(start, count, run, 0)

    def at_ctx(by):
        return (lax.rem(me + by + n_ctx, n_ctx), head)

    def at_head(by):
        return (me, lax.rem(head + by + n_head, n_head))

    def send(src, dst, s_sem, r_sem, where):
        return pltpu.make_async_remote_copy(
            src_ref=src, dst_ref=dst, send_sem=s_sem, recv_sem=r_sem, device_id=where, device_id_type=MESH
        )

    loop(chunks, lambda i: load_g(i).start())

    away_by = sorted({by % n_ctx for o in offset_list[1:] for by in (o, -o)})
    barrier = pltpu.get_barrier_semaphore()
    for by in away_by:
        pl.semaphore_signal(barrier, inc=1, device_id=at_ctx(by), device_id_type=MESH)
    for j in range(1, n_head):
        pl.semaphore_signal(barrier, inc=1, device_id=at_head(j), device_id_type=MESH)
    pl.semaphore_wait(barrier, len(away_by) + n_head - 1)

    gather = [
        send(kv_ref, kvbuf.at[pos, 0], gs_s.at[pos - 1], gs_r.at[pos - 1], at_ctx(offset_list[pos]))
        for pos in range(1, n_off)
    ]
    spread = [
        [
            send(kv_ref if pos == 0 else kvbuf.at[pos, 0], kvbuf.at[pos, j],
                 fw_s.at[pos, j - 1], fw_r.at[pos, j - 1], at_head(-j))
            for j in range(1, n_head)
        ]
        for pos in range(n_off)
    ]
    for copy in [gather[0]] + gather[:0:-1]:
        copy.start()
    for copy in spread[0]:
        copy.start()
    loop(steps, lambda i: load_q(i).start())
    kvbuf[0, 0] = kv_ref[...]

    def relayout(i):
        load_g(i).wait()
        wide = graw[i].reshape(width * heads, lat).astype(F32)
        lanes = gwide.shape[2]
        for c in range(gwide.shape[0]):
            gwide[c] = wide[:, c * lanes : (c + 1) * lanes]
        for h in range(heads):
            for c in range(gwide.shape[0]):
                gv[h // group, h % group, pl.ds(i * width, width), c * lanes : (c + 1) * lanes] = gwide[
                    c, pl.ds(h, width, stride=heads), :
                ].astype(BF16)

    loop(chunks - 1, relayout)

    def scores(i, low, high):
        keys = kvbuf[low:high].reshape((high - low) * blk, feat)
        q = jnp.concatenate([qv[i, k] for k in range(group)], 1)
        g = gv[i].reshape(cols, lat)
        ln = jnp.concatenate([ln_ref[i, k : k + 1, :] for k in range(group)], 1) * log2e
        od = jnp.concatenate([od_ref[i, k : k + 1, :] for k in range(group)], 1)
        s = dot(keys, q, 1, 0)
        dp = dot(keys[:, :lat], g, 1, 1)
        ps, dss = [], []
        for pos in range(low, high):
            sl = slice((pos - low) * blk, (pos - low + 1) * blk)
            bias = jnp.where(links[0, pos] > 0, ln, 1e30)
            p = jnp.exp2(s[sl] * (scale * log2e) - bias)
            if offset_list[pos] == 0:
                key = lax.broadcasted_iota(jnp.int32, p.shape, 0) + head * part
                key = jnp.where(key >= blk, key - blk, key)
                tok = lax.rem(lax.broadcasted_iota(jnp.int32, p.shape, 1), toks)
                p = jnp.where(tok >= key, p, 0.0)
            ps.append(p.astype(BF16))
            dss.append((p * (dp[sl] - od) * scale).astype(BF16))
        return jnp.concatenate(ps, 0), jnp.concatenate(dss, 0), q, g

    def key_terms(pb, ds, q, g, low, high):
        rows = slice(low * blk, high * blk)
        dk = dot(ds, q, 1, 1)
        dv = dot(pb, g, 1, 0)
        acc[rows, :lat] += dk[:, :lat] + dv
        acc[rows, lat:] += dk[:, lat:]

    def across(low, high, slot):
        return [
            send(away.at[j - 1, low:high], yrecv.at[j - 1, low:high], ry_s.at[slot, j - 1],
                 ry_r.at[slot, j - 1], at_head(j))
            for j in range(1, n_head)
        ]

    def pack(low, high):
        for pos in range(low, high):
            for j in range(1, n_head):
                start = pos * blk + j * part
                away[j - 1, pos] = acc[start : start + part, :].astype(BF16)

    def folded(pos):
        total = acc[pos * blk : pos * blk + part, :]
        for j in range(1, n_head):
            total = total + yrecv[j - 1, pos].astype(F32)
        return total

    back = [
        send(fwd.at[pos - 1], crecv.at[pos - 1], rc_s.at[pos - 1], rc_r.at[pos - 1], at_ctx(-offset_list[pos]))
        for pos in range(1, n_off)
    ]

    acc[...] = jnp.zeros_like(acc)

    def onward(low, high):
        for pos in range(low, high):
            gather[pos - 1].wait_recv()
            for copy in spread[pos]:
                copy.start()

    def arrive(low, high):
        for pos in range(low, high):
            for copy in spread[pos]:
                copy.wait_recv()

    def first(i):
        load_q(i).wait()
        pb, ds, _, _ = scores(i, *FIRST)
        dsv[i, : FIRST[1] * blk, :] = ds
        pbv[i] = pb

    onward(1, FIRST[1])
    loop(chunks, relayout, chunks - 1)
    arrive(*FIRST)
    loop(steps // 2, first)
    onward(*LAST)
    loop(steps, first, steps // 2)
    arrive(*LAST)

    def second(i):
        pb, ds, q, g = scores(i, *LAST)
        dsv[i, LAST[0] * blk : LAST[1] * blk, :] = ds
        key_terms(pb, ds, q, g, *LAST)

    loop(steps, second)
    pack(*LAST)

    def third(i):
        q = jnp.concatenate([qv[i, k] for k in range(group)], 1)
        key_terms(pbv[i], dsv[i, : FIRST[1] * blk, :], q, gv[i].reshape(cols, lat), *FIRST)

    def fourth(i):
        keys = kvbuf[...].reshape(n_off * blk, feat)
        dq = dot(keys, dsv[i], 0, 0).astype(BF16)
        for k in range(group):
            dqv[i, k] = dq[:, k * toks : (k + 1) * toks]

    far, near = across(*LAST, 1), across(*FIRST, 0)
    for copy in far:
        copy.start()
    loop(steps, third)
    for copy in far:
        copy.wait_recv()
    for pos in range(*LAST):
        fwd[pos - 1] = folded(pos).astype(BF16)
    pack(*FIRST)
    for pos in range(*LAST):
        back[pos - 1].start()
    for copy in near:
        copy.start()
    loop(steps, fourth)
    for copy in near:
        copy.wait_recv()
    for pos in range(1, FIRST[1]):
        fwd[pos - 1] = folded(pos).astype(BF16)
    total = folded(0)
    for pos in range(1, FIRST[1]):
        back[pos - 1].start()
    for copy in gather + sum(spread, []) + far + near:
        copy.wait_send()
    for copy in back[::-1]:
        copy.wait()
    for pos in range(1, n_off):
        total = total + crecv[pos - 1].astype(F32)
    dkv_ref[...] = total.astype(BF16)


def fused(n_ctx, n_head, q, g, ln, od, kv, links, group=4, width=32):
    heads, feat, toks = q.shape
    lat = g.shape[2]
    part = kv.shape[0]
    n_off = len(offset_list)
    group = math.gcd(group, heads)
    width = math.gcd(width, toks)
    steps, chunks = heads // group, toks // width
    cols, keys = group * toks, n_off * n_head * part
    near = FIRST[1] * n_head * part
    dma = pltpu.SemaphoreType.DMA
    hbm = pl.BlockSpec(memory_space=pl.ANY)
    vmem = pl.BlockSpec(memory_space=pltpu.VMEM)
    return pl.pallas_call(
        functools.partial(fused_kernel, n_ctx, n_head),
        in_specs=[pl.BlockSpec(memory_space=pltpu.SMEM), vmem, hbm, hbm, vmem, vmem],
        out_specs=[vmem, vmem],
        out_shape=[
            pltpu.VMEM((steps, group, feat, toks), BF16),
            jax.ShapeDtypeStruct((part, feat), BF16),
        ],
        scratch_shapes=[
            pltpu.VMEM((steps, group, feat, toks), BF16),
            pltpu.VMEM((chunks, width, heads, lat), BF16),
            pltpu.VMEM((lat // 128, width * heads, 128), F32),
            pltpu.VMEM((steps, group, toks, lat), BF16),
            pltpu.VMEM((steps, keys, cols), BF16),
            pltpu.VMEM((steps, near, cols), BF16),
            pltpu.VMEM((keys, feat), F32),
            pltpu.VMEM((n_off, n_head, part, feat), BF16),
            pltpu.VMEM((n_head - 1, n_off, part, feat), BF16),
            pltpu.VMEM((n_head - 1, n_off, part, feat), BF16),
            pltpu.VMEM((n_off - 1, part, feat), BF16),
            pltpu.VMEM((n_off - 1, part, feat), BF16),
            dma((steps,)),
            dma((chunks,)),
            dma((n_off - 1,)),
            dma((n_off - 1,)),
            dma((n_off, n_head - 1)),
            dma((n_off, n_head - 1)),
            dma((2, n_head - 1)),
            dma((2, n_head - 1)),
            dma((n_off - 1,)),
            dma((n_off - 1,)),
        ],
        compiler_params=pltpu.CompilerParams(
            collective_id=0, has_side_effects=True, vmem_limit_bytes=67043328 - 2 * heads * feat * toks - 16384
        ),
        cost_estimate=pl.CostEstimate(flops=12 * 10**9, bytes_accessed=14 * 10**6, transcendentals=2 * 10**6),
        name="mla_bwd",
    )(links, kv, q, g, ln.reshape(steps, group, toks), od.reshape(steps, group, toks))


def shards(q, g, ln, od, kv, links):
    dq, dkv = fused(
        lax.axis_size("ctx"),
        lax.axis_size("head"),
        jnp.transpose(q, (1, 2, 0)),
        g,
        ln.T,
        od.T,
        kv,
        links,
    )
    return jnp.transpose(dq.reshape(-1, *dq.shape[2:]), (2, 0, 1)), dkv


def solution(mesh):
    in_specs = (
        P("ctx", "head", None),
        P("ctx", "head", None),
        P("ctx", "head"),
        P("ctx", "head"),
        P(("ctx", "head"), None),
        P("ctx", None),
    )
    out_specs = (P("ctx", "head", None), P(("ctx", "head"), None))
    return jax.shard_map(shards, mesh=mesh, in_specs=in_specs, out_specs=out_specs, check_vma=False)
```

```python
import functools
import math

import jax
import jax.numpy as jnp
from jax import lax
from jax.experimental import pallas as pl
from jax.experimental.pallas import tpu as pltpu
from jax.sharding import PartitionSpec as P

offset_list = (0, 1, 2, 8)
F32 = jnp.float32
BF16 = jnp.bfloat16


def dot(a, b, ca, cb):
    return lax.dot_general(a, b, (((ca,), (cb,)), ((), ())), preferred_element_type=F32)


MESH = pl.DeviceIdType.MESH
FIRST, LAST = (0, 2), (2, 4)


def fused_kernel(
    n_ctx, n_head, links, kv_ref, q_hbm, g_hbm, ln_ref, od_ref,
    dqv, dkv_ref,
    qv, graw, gwide, gv, dsv, pbv, acc, kvbuf, away, yrecv, fwd, crecv,
    q_sem, g_sem, gs_s, gs_r, fw_s, fw_r, ry_s, ry_r, rc_s, rc_r,
):
    me = lax.axis_index("ctx")
    head = lax.axis_index("head")
    steps, group, feat, toks = qv.shape
    chunks, width, heads, lat = graw.shape
    cols = group * toks
    n_off, _, part, _ = kvbuf.shape
    blk = n_head * part
    scale = feat ** (-0.5)
    log2e = math.log2(math.e)

    def load_g(i):
        return pltpu.make_async_copy(g_hbm.at[pl.ds(i * width, width)], graw.at[i], g_sem.at[i])

    def load_q(i):
        return pltpu.make_async_copy(q_hbm.at[pl.ds(i * group, group)], qv.at[i], q_sem.at[i])

    def loop(count, body, start=0):
        def run(i, carry):
            body(i)
            return carry

        lax.fori_loop(start, count, run, 0)

    def at_ctx(by):
        return (lax.rem(me + by + n_ctx, n_ctx), head)

    def at_head(by):
        return (me, lax.rem(head + by + n_head, n_head))

    def send(src, dst, s_sem, r_sem, where):
        return pltpu.make_async_remote_copy(
            src_ref=src, dst_ref=dst, send_sem=s_sem, recv_sem=r_sem, device_id=where, device_id_type=MESH
        )

    loop(chunks, lambda i: load_g(i).start())

    away_by = sorted({by % n_ctx for o in offset_list[1:] for by in (o, -o)})
    barrier = pltpu.get_barrier_semaphore()
    for by in away_by:
        pl.semaphore_signal(barrier, inc=1, device_id=at_ctx(by), device_id_type=MESH)
    for j in range(1, n_head):
        pl.semaphore_signal(barrier, inc=1, device_id=at_head(j), device_id_type=MESH)
    pl.semaphore_wait(barrier, len(away_by) + n_head - 1)

    gather = [
        send(kv_ref, kvbuf.at[pos, 0], gs_s.at[pos - 1], gs_r.at[pos - 1], at_ctx(offset_list[pos]))
        for pos in range(1, n_off)
    ]
    spread = [
        [
            send(kv_ref if pos == 0 else kvbuf.at[pos, 0], kvbuf.at[pos, j],
                 fw_s.at[pos, j - 1], fw_r.at[pos, j - 1], at_head(-j))
            for j in range(1, n_head)
        ]
        for pos in range(n_off)
    ]
    for copy in [gather[0]] + gather[:0:-1]:
        copy.start()
    for copy in spread[0]:
        copy.start()
    loop(steps, lambda i: load_q(i).start())
    kvbuf[0, 0] = kv_ref[...]

    def relayout(i):
        load_g(i).wait()
        wide = graw[i].reshape(width * heads, lat).astype(F32)
        lanes = gwide.shape[2]
        for c in range(gwide.shape[0]):
            gwide[c] = wide[:, c * lanes : (c + 1) * lanes]
        for h in range(heads):
            for c in range(gwide.shape[0]):
                gv[h // group, h % group, pl.ds(i * width, width), c * lanes : (c + 1) * lanes] = gwide[
                    c, pl.ds(h, width, stride=heads), :
                ].astype(BF16)

    loop(chunks - 1, relayout)

    def scores(i, low, high):
        keys = kvbuf[low:high].reshape((high - low) * blk, feat)
        q = jnp.concatenate([qv[i, k] for k in range(group)], 1)
        g = gv[i].reshape(cols, lat)
        ln = jnp.concatenate([ln_ref[i, k : k + 1, :] for k in range(group)], 1) * log2e
        od = jnp.concatenate([od_ref[i, k : k + 1, :] for k in range(group)], 1)
        s = dot(keys, q, 1, 0)
        dp = dot(keys[:, :lat], g, 1, 1)
        ps, dss = [], []
        for pos in range(low, high):
            sl = slice((pos - low) * blk, (pos - low + 1) * blk)
            bias = jnp.where(links[0, pos] > 0, ln, 1e30)
            p = jnp.exp2(s[sl] * (scale * log2e) - bias)
            if offset_list[pos] == 0:
                key = lax.broadcasted_iota(jnp.int32, p.shape, 0) + head * part
                key = jnp.where(key >= blk, key - blk, key)
                tok = lax.rem(lax.broadcasted_iota(jnp.int32, p.shape, 1), toks)
                p = jnp.where(tok >= key, p, 0.0)
            ps.append(p.astype(BF16))
            dss.append((p * (dp[sl] - od) * scale).astype(BF16))
        return jnp.concatenate(ps, 0), jnp.concatenate(dss, 0), q, g

    def key_terms(pb, ds, q, g, low, high):
        rows = slice(low * blk, high * blk)
        dk = dot(ds, q, 1, 1)
        dv = dot(pb, g, 1, 0)
        acc[rows, :lat] += dk[:, :lat] + dv
        acc[rows, lat:] += dk[:, lat:]

    def across(low, high, slot):
        return [
            send(away.at[j - 1, low:high], yrecv.at[j - 1, low:high], ry_s.at[slot, j - 1],
                 ry_r.at[slot, j - 1], at_head(j))
            for j in range(1, n_head)
        ]

    def pack(low, high):
        for pos in range(low, high):
            for j in range(1, n_head):
                start = pos * blk + j * part
                away[j - 1, pos] = acc[start : start + part, :].astype(BF16)

    def folded(pos):
        total = acc[pos * blk : pos * blk + part, :]
        for j in range(1, n_head):
            total = total + yrecv[j - 1, pos].astype(F32)
        return total

    back = [
        send(fwd.at[pos - 1], crecv.at[pos - 1], rc_s.at[pos - 1], rc_r.at[pos - 1], at_ctx(-offset_list[pos]))
        for pos in range(1, n_off)
    ]

    acc[...] = jnp.zeros_like(acc)

    def onward(low, high):
        for pos in range(low, high):
            gather[pos - 1].wait_recv()
            for copy in spread[pos]:
                copy.start()

    def arrive(low, high):
        for pos in range(low, high):
            for copy in spread[pos]:
                copy.wait_recv()

    def first(i):
        load_q(i).wait()
        pb, ds, _, _ = scores(i, *FIRST)
        dsv[i, : FIRST[1] * blk, :] = ds
        pbv[i] = pb

    onward(1, FIRST[1])
    loop(chunks, relayout, chunks - 1)
    arrive(*FIRST)
    loop(steps // 2, first)
    onward(*LAST)
    loop(steps, first, steps // 2)
    arrive(*LAST)

    def second(i):
        pb, ds, q, g = scores(i, *LAST)
        dsv[i, LAST[0] * blk : LAST[1] * blk, :] = ds
        key_terms(pb, ds, q, g, *LAST)

    loop(steps, second)
    pack(*LAST)

    def third(i):
        q = jnp.concatenate([qv[i, k] for k in range(group)], 1)
        key_terms(pbv[i], dsv[i, : FIRST[1] * blk, :], q, gv[i].reshape(cols, lat), *FIRST)

    def fourth(i):
        keys = kvbuf[...].reshape(n_off * blk, feat)
        dq = dot(keys, dsv[i], 0, 0).astype(BF16)
        for k in range(group):
            dqv[i, k] = dq[:, k * toks : (k + 1) * toks]

    far, near = across(*LAST, 1), across(*FIRST, 0)
    for copy in far:
        copy.start()
    loop(steps, third)
    for copy in far:
        copy.wait_recv()
    for pos in range(*LAST):
        fwd[pos - 1] = folded(pos).astype(BF16)
    pack(*FIRST)
    for pos in range(*LAST):
        back[pos - 1].start()
    for copy in near:
        copy.start()
    loop(steps, fourth)
    for copy in near:
        copy.wait_recv()
    for pos in range(1, FIRST[1]):
        fwd[pos - 1] = folded(pos).astype(BF16)
    total = folded(0)
    for pos in range(1, FIRST[1]):
        back[pos - 1].start()
    for copy in gather + sum(spread, []) + far + near:
        copy.wait_send()
    for copy in back[::-1]:
        copy.wait()
    for pos in range(1, n_off):
        total = total + crecv[pos - 1].astype(F32)
    dkv_ref[...] = total.astype(BF16)


def fused(n_ctx, n_head, q, g, ln, od, kv, links, group=8, width=32):
    heads, feat, toks = q.shape
    lat = g.shape[2]
    part = kv.shape[0]
    n_off = len(offset_list)
    group = math.gcd(group, heads)
    width = math.gcd(width, toks)
    steps, chunks = heads // group, toks // width
    cols, keys = group * toks, n_off * n_head * part
    near = FIRST[1] * n_head * part
    dma = pltpu.SemaphoreType.DMA
    hbm = pl.BlockSpec(memory_space=pl.ANY)
    vmem = pl.BlockSpec(memory_space=pltpu.VMEM)
    return pl.pallas_call(
        functools.partial(fused_kernel, n_ctx, n_head),
        in_specs=[pl.BlockSpec(memory_space=pltpu.SMEM), vmem, hbm, hbm, vmem, vmem],
        out_specs=[vmem, vmem],
        out_shape=[
            pltpu.VMEM((steps, group, feat, toks), BF16),
            jax.ShapeDtypeStruct((part, feat), BF16),
        ],
        scratch_shapes=[
            pltpu.VMEM((steps, group, feat, toks), BF16),
            pltpu.VMEM((chunks, width, heads, lat), BF16),
            pltpu.VMEM((lat // 128, width * heads, 128), F32),
            pltpu.VMEM((steps, group, toks, lat), BF16),
            pltpu.VMEM((steps, keys, cols), BF16),
            pltpu.VMEM((steps, near, cols), BF16),
            pltpu.VMEM((keys, feat), F32),
            pltpu.VMEM((n_off, n_head, part, feat), BF16),
            pltpu.VMEM((n_head - 1, n_off, part, feat), BF16),
            pltpu.VMEM((n_head - 1, n_off, part, feat), BF16),
            pltpu.VMEM((n_off - 1, part, feat), BF16),
            pltpu.VMEM((n_off - 1, part, feat), BF16),
            dma((steps,)),
            dma((chunks,)),
            dma((n_off - 1,)),
            dma((n_off - 1,)),
            dma((n_off, n_head - 1)),
            dma((n_off, n_head - 1)),
            dma((2, n_head - 1)),
            dma((2, n_head - 1)),
            dma((n_off - 1,)),
            dma((n_off - 1,)),
        ],
        compiler_params=pltpu.CompilerParams(
            collective_id=0, has_side_effects=True, vmem_limit_bytes=67043328 - 2 * heads * feat * toks - 16384
        ),
        cost_estimate=pl.CostEstimate(flops=12 * 10**9, bytes_accessed=14 * 10**6, transcendentals=2 * 10**6),
        name="mla_bwd",
    )(links, kv, q, g, ln.reshape(steps, group, toks), od.reshape(steps, group, toks))


def shards(q, g, ln, od, kv, links):
    dq, dkv = fused(
        lax.axis_size("ctx"),
        lax.axis_size("head"),
        jnp.transpose(q, (1, 2, 0)),
        g,
        ln.T,
        od.T,
        kv,
        links,
    )
    return jnp.transpose(dq.reshape(-1, *dq.shape[2:]), (2, 0, 1)), dkv


def solution(mesh):
    in_specs = (
        P("ctx", "head", None),
        P("ctx", "head", None),
        P("ctx", "head"),
        P("ctx", "head"),
        P(("ctx", "head"), None),
        P("ctx", None),
    )
    out_specs = (P("ctx", "head", None), P(("ctx", "head"), None))
    return jax.shard_map(shards, mesh=mesh, in_specs=in_specs, out_specs=out_specs, check_vma=False)
```
